128 devices in a mesh: cuts: 2 (over y_hi), fsdp: 8 (over z, core), tensor: 8 (over x, y_lo).
Axes of the slice: x: 4, y: 4 (y_hi: 2, y_lo: 2; y = y_hi * 2 + y_lo), z: 4, core: 2. Of those that a mesh axis runs over, the one named last changes fastest.
Arguments:
- tokens: bfloat16 [1536, 6144], P(('cuts', 'fsdp'), 'tensor'), may hold values from -6 to 6
- w_in: bfloat16 [6144, 24576], P('tensor', 'fsdp'), may hold values from -0.078125 to 0.078125
- w_out: bfloat16 [24576, 6144], P('fsdp', 'tensor'), may hold values from -0.078125 to 0.078125
- cotangent: bfloat16 [1536, 6144], P(('cuts', 'fsdp'), 'tensor'), may hold values from -6 to 6
Outputs:
- mixed: bfloat16 [1536, 6144], P(('cuts', 'fsdp'), 'tensor')
- token_grad: bfloat16 [1536, 6144], P(('cuts', 'fsdp'), 'tensor')
- in_grad: bfloat16 [6144, 24576], P('tensor', 'fsdp')
- out_grad: bfloat16 [24576, 6144], P('fsdp', 'tensor')
The draws below stay inside these ranges and needn't reach their ends.
All inputs are finite; a program needn't handle non-finite values.
Results may differ from the reference program's by a relative error of at most 0.025.
Values may be sent and summed in bfloat16 or wider, within the bound.
No kernel may reach another device: no remote copies, remote signals or barrier semaphores. Data moves between devices by JAX's collectives and lax.ppermute only.
A program may use at most 128 MiB of HBM per device.

```python
import jax
import jax.numpy as jnp
from jax import lax

D = 6144
FF = 24576
TOKENS = 1536
N_CUTS = 2
N_FSDP = 8
N_TENSOR = 8


def block_levels(stream_key, shape, shards, least, top_value):
    level = 1.0
    for axis_at, blocks in shards:
        heights = jax.random.uniform(jax.random.fold_in(jax.random.fold_in(stream_key, 6), axis_at), (blocks,), jnp.float32, least / len(shards), top_value / len(shards))
        level = level * jnp.repeat(jnp.exp(heights), shape[axis_at] // blocks).reshape((-1,) + (1,) * (len(shape) - 1 - axis_at))
    return level


def scatter_about(rng, dims, deviation, reach, shards=(), kind=jnp.bfloat16):
    array = deviation * jax.random.normal(rng, dims, jnp.float32)
    if shards:
        array = array * block_levels(rng, dims, shards, -0.22, 0.18)
    return jnp.clip(array, -reach, reach).astype(kind)


def setup_inputs(seed: int = 0) -> dict:
    seeds = jax.random.split(jax.random.key(seed), 5)
    return {
        "tokens": scatter_about(seeds[0], (TOKENS, D), 1.0, 6.0, ((0, 16), (1, 8))),
        "w_in": scatter_about(seeds[1], (D, FF), D ** -0.5, 0.078125, ((0, 8), (1, 8))),
        "w_out": scatter_about(seeds[2], (FF, D), (FF // 4) ** -0.5, 0.078125, ((0, 8), (1, 8))),
        "cotangent": scatter_about(seeds[3], (TOKENS, D), 1.0, 6.0, ((0, 16), (1, 8))),
    }


root_coef = 0.7978845608
cube_coef = 0.044715


def gelu_value(pre_act):
    tanh_part = jnp.tanh(root_coef * (pre_act + cube_coef * pre_act * pre_act * pre_act))
    return 0.5 * pre_act * (1.0 + tanh_part)


def gelu_slope(pre_act):
    tanh_part = jnp.tanh(root_coef * (pre_act + cube_coef * pre_act * pre_act * pre_act))
    return 0.5 * (1.0 + tanh_part) + 0.5 * pre_act * (1.0 - tanh_part * tanh_part) * root_coef * (1.0 + 3.0 * cube_coef * pre_act * pre_act)


def rounded(values):
    return lax.optimization_barrier(values.astype(jnp.bfloat16)).astype(jnp.float32)


def reference(tokens, w_in, w_out, cotangent):
    slice_rows = TOKENS // N_CUTS
    width_part = D // N_TENSOR
    hidden_part = FF // N_FSDP
    mixed_list = []
    token_list = []
    in_total = jnp.zeros((D, FF), jnp.float32)
    out_total = jnp.zeros((FF, D), jnp.float32)
    for group in range(N_CUTS):
        rows_here = tokens[group * slice_rows:(group + 1) * slice_rows]
        cot_here = cotangent[group * slice_rows:(group + 1) * slice_rows]
        pre_act = jnp.zeros((slice_rows, FF), jnp.float32)
        act_grad = jnp.zeros((slice_rows, FF), jnp.float32)
        for block in range(N_TENSOR):
            low = block * width_part
            pre_act = pre_act + rounded(jnp.dot(rows_here[:, low:low + width_part], w_in[low:low + width_part], preferred_element_type=jnp.float32))
            act_grad = act_grad + rounded(jnp.dot(cot_here[:, low:low + width_part], w_out[:, low:low + width_part].T, preferred_element_type=jnp.float32))
        act = gelu_value(pre_act).astype(jnp.bfloat16)
        pre_grad = (act_grad * gelu_slope(pre_act)).astype(jnp.bfloat16)
        mixed_sum = jnp.zeros((slice_rows, D), jnp.float32)
        token_sum = jnp.zeros((slice_rows, D), jnp.float32)
        for block in range(N_FSDP):
            low = block * hidden_part
            mixed_sum = mixed_sum + rounded(jnp.dot(act[:, low:low + hidden_part], w_out[low:low + hidden_part], preferred_element_type=jnp.float32))
            token_sum = token_sum + rounded(jnp.dot(pre_grad[:, low:low + hidden_part], w_in[:, low:low + hidden_part].T, preferred_element_type=jnp.float32))
        mixed_list.append(mixed_sum.astype(jnp.bfloat16))
        token_list.append(token_sum.astype(jnp.bfloat16))
        out_total = out_total + rounded(jnp.dot(act.T, cot_here, preferred_element_type=jnp.float32))
        in_total = in_total + rounded(jnp.dot(rows_here.T, pre_grad, preferred_element_type=jnp.float32))
    mixed = jnp.concatenate(mixed_list, axis=0)
    token_grad = jnp.concatenate(token_list, axis=0)
    return mixed, token_grad, in_total.astype(jnp.bfloat16), out_total.astype(jnp.bfloat16)
```

```python
import jax
import jax.numpy as jnp
from jax import lax
from jax.sharding import PartitionSpec as P

root_coef = 0.7978845608
cube_coef = 0.044715
AXES = ("cuts", "fsdp", "tensor")
bf16 = jnp.bfloat16
f32 = jnp.float32


def place(index):
    c, rest = divmod(index, 64)
    f, t = divmod(rest, 8)
    x, low = divmod(t, 2)
    z, core = divmod(f, 2)
    return x, 2 * c + low, z, core


def index_of(x, y, z, core):
    return (y // 2) * 64 + (2 * z + core) * 8 + 2 * x + y % 2


def partner(dx=0, dy=0, dz=0, dcore=0):
    pairs = []
    for i in range(128):
        x, y, z, core = place(i)
        pairs.append((i, index_of(x ^ dx, y ^ dy, z ^ dz, core ^ dcore)))
    return pairs


def swap(value, name, **step):
    with jax.named_scope(name):
        return lax.ppermute(value, AXES, partner(**step))


x_rings = sorted({tuple(index_of(s, *place(i)[1:]) for s in range(4)) for i in range(128)})


def x_exchange(blocks):
    return lax.all_to_all(blocks, AXES, 0, 0, axis_index_groups=[list(r) for r in x_rings], tiled=True)


def gelu_both(pre_act):
    tanh_part = jnp.tanh(root_coef * (pre_act + cube_coef * pre_act * pre_act * pre_act))
    value = 0.5 * pre_act * (1.0 + tanh_part)
    slope = 0.5 * (1.0 + tanh_part) + 0.5 * pre_act * (1.0 - tanh_part * tanh_part) * root_coef * (
        1.0 + 3.0 * cube_coef * pre_act * pre_act
    )
    return value, slope


def product(left, right, dims):
    return lax.dot_general(left, right, (dims, ((), ())), preferred_element_type=f32).astype(bf16)


def gather_y(rows, name):
    a = swap(rows, name + "_y1", dy=1)
    b = swap(rows, name + "_y3", dy=3)
    d = swap(rows, name + "_y2", dy=2)
    return jnp.concatenate(
        [jnp.concatenate([rows, a], 1), jnp.concatenate([d, b], 1)], 0
    )


def gather_z(rows, name):
    parts = [rows[None]] + [swap(rows, name + f"_z{j}", dz=j)[None] for j in (1, 3, 2)]
    own = jnp.concatenate([parts[0], parts[1], parts[3], parts[2]], 0)
    other = swap(own, name + "_core", dcore=1)
    return jnp.concatenate([own, other], 1).reshape(1536, 1536)


def reduce_out(partial, name):
    blocks = partial.reshape(4, 2, 192, 1536)
    got = swap(blocks[:, 1], name + "_core", dcore=1)
    total = (blocks[:, 0].astype(f32) + got.astype(f32)).astype(bf16)
    parts = [swap(total[j], name + f"_z{j}", dz=j) for j in (1, 3, 2)]
    rows = total[0].astype(f32) + sum(p.astype(f32) for p in parts)
    kept = rows[:96, :768]
    rows = rows.astype(bf16)
    a = swap(rows[:96, 768:], name + "_y1", dy=1)
    b = swap(rows[96:, 768:], name + "_y3", dy=3)
    d = swap(rows[96:, :768], name + "_y2", dy=2)
    return (kept + a.astype(f32) + b.astype(f32) + d.astype(f32)).astype(bf16)


def local(tokens, w_in, w_out, cotangent):
    y = 2 * lax.axis_index("cuts") + lax.axis_index("tensor") % 2
    y1, y2, y3 = y ^ 1, y ^ 2, y ^ 3

    tok_y = gather_y(tokens, "tok")
    in_a = swap(lax.dynamic_slice(w_in, (0, y1 * 768), (384, 768)), "win_y1", dy=1)
    in_b = swap(lax.dynamic_slice(w_in, (384, y3 * 768), (384, 768)), "win_y3", dy=3)
    tok = gather_z(tok_y, "tok")
    w1 = jnp.concatenate([lax.dynamic_slice(w_in, (0, y * 768), (768, 768)), in_a, in_b], 0)

    cot_y = gather_y(cotangent, "cot")
    out_a = swap(lax.dynamic_slice(w_out, (y1 * 768, 0), (384, 768)), "wout_y1", dy=1)
    out_b = swap(lax.dynamic_slice(w_out, (y3 * 768 + 384, 0), (384, 768)), "wout_y3", dy=3)
    cot = gather_z(cot_y, "cot")
    w2 = jnp.concatenate(
        [lax.dynamic_slice(w_out, (y * 768, 0), (768, 768)), jnp.concatenate([out_a, out_b], 0)], 1
    )

    pre = x_exchange(product(tok, w1, ((1,), (0,))))
    pre_act = jnp.sum(pre.reshape(4, 384, 768).astype(f32), 0)
    act_own, slope = gelu_both(pre_act)
    act_own = act_own.astype(bf16)
    act = x_exchange(jnp.broadcast_to(act_own, (4, 384, 768)).reshape(1536, 768))

    out_far = product(act, cot[:, 768:], ((0,), (0,)))
    og_a = swap(out_far, "og_y1", dy=1)
    og_b = swap(out_far, "og_y3", dy=3)
    out_near = product(act, cot[:, :768], ((0,), (0,)))
    og_d = swap(out_near, "og_y2", dy=2)

    back = x_exchange(product(cot, w2, ((1,), (1,))))
    act_grad = jnp.sum(back.reshape(4, 384, 768).astype(f32), 0)
    pre_grad_own = (act_grad * slope).astype(bf16)
    pre_grad = x_exchange(jnp.broadcast_to(pre_grad_own, (4, 384, 768)).reshape(1536, 768))

    in_far = product(tok[:, 768:], pre_grad, ((0,), (0,)))
    ig_a = swap(in_far, "ig_y1", dy=1)
    ig_b = swap(in_far, "ig_y3", dy=3)
    in_near = product(tok[:, :768], pre_grad, ((0,), (0,)))
    ig_d = swap(in_near, "ig_y2", dy=2)

    mixed = reduce_out(product(act, w2, ((1,), (0,))), "mix")
    token_grad = reduce_out(product(pre_grad, w1, ((1,), (1,))), "tg")

    out_grad = jnp.zeros((3072, 768), bf16)
    for piece, at in ((out_near, y), (og_a, y1), (og_b, y3), (og_d, y2)):
        out_grad = lax.dynamic_update_slice(out_grad, piece, (at * 768, 0))
    in_grad = jnp.zeros((768, 3072), bf16)
    for piece, at in ((in_near, y), (ig_a, y1), (ig_b, y3), (ig_d, y2)):
        in_grad = lax.dynamic_update_slice(in_grad, piece, (0, at * 768))
    return mixed, token_grad, in_grad, out_grad


def solution(mesh):
    rows = P(("cuts", "fsdp"), "tensor")
    specs = (rows, P("tensor", "fsdp"), P("fsdp", "tensor"), rows)
    outs = (rows, rows, P("tensor", "fsdp"), P("fsdp", "tensor"))
    return jax.shard_map(local, mesh=mesh, in_specs=specs, out_specs=outs, check_vma=False)
```

```python
import jax
import jax.numpy as jnp
from jax import lax
from jax.experimental import pallas as pl
from jax.experimental.pallas import tpu as pltpu
from jax.sharding import PartitionSpec as P


root_coef = 0.7978845608
cube_coef = 0.044715
AXES = ("cuts", "fsdp", "tensor")
bf16 = jnp.bfloat16
f32 = jnp.float32


def place(index):
    c, rest = divmod(index, 64)
    f, t = divmod(rest, 8)
    x, low = divmod(t, 2)
    z, core = divmod(f, 2)
    return x, 2 * c + low, z, core


def index_of(x, y, z, core):
    return (y // 2) * 64 + (2 * z + core) * 8 + 2 * x + y % 2


def partner(dx=0, dy=0, dz=0, dcore=0):
    pairs = []
    for i in range(128):
        x, y, z, core = place(i)
        pairs.append((i, index_of(x ^ dx, y ^ dy, z ^ dz, core ^ dcore)))
    return pairs


def swap(value, **step):
    return lax.ppermute(value, AXES, partner(**step))


def swap_x(values):
    got = {j: swap(values[j], dx=j) for j in (1, 3, 2)}
    return [got[j] for j in (1, 2, 3)]


def gelu_both(pre_act):
    tanh_part = jnp.tanh(root_coef * (pre_act + cube_coef * pre_act * pre_act * pre_act))
    value = 0.5 * pre_act * (1.0 + tanh_part)
    slope = 0.5 * (1.0 + tanh_part) + 0.5 * pre_act * (1.0 - tanh_part * tanh_part) * root_coef * (
        1.0 + 3.0 * cube_coef * pre_act * pre_act
    )
    return value, slope


def my_y():
    return 2 * lax.axis_index("cuts") + lax.axis_index("tensor") % 2


def my_x():
    return lax.axis_index("tensor") // 2


HBM = pl.BlockSpec(memory_space=pltpu.HBM)


def call(body, args, outs, scratch, flops, aliases=None):
    size = sum(v.size * 2 for v in (*args, *outs))
    return pl.pallas_call(
        body,
        out_shape=outs,
        in_specs=[HBM] * len(args),
        out_specs=[HBM] * len(outs),
        scratch_shapes=scratch,
        input_output_aliases=aliases or {},
        compiler_params=pltpu.CompilerParams(vmem_limit_bytes=67043328),
        cost_estimate=pl.CostEstimate(flops=flops, transcendentals=0, bytes_accessed=size),
    )(*args)


def fetch(pairs, sem):
    for source, target in pairs:
        pltpu.make_async_copy(source, target, sem).start()


def arrived(ref, sem):
    pltpu.make_async_copy(ref, ref, sem).wait()


def weight_parts(kind, refs, store):
    whole, a, b = refs
    at = pl.multiple_of(my_y() * 768, 768)
    if kind == "in":
        return [
            (whole.at[:, pl.ds(at, 768)], store.at[pl.ds(0, 768), :]),
            (a, store.at[pl.ds(768, 384), :]),
            (b, store.at[pl.ds(1152, 384), :]),
        ]
    return [
        (whole.at[pl.ds(at, 768), :], store.at[:, pl.ds(0, 768)]),
        (a, store.at[pl.ds(0, 384), pl.ds(768, 768)]),
        (b, store.at[pl.ds(384, 384), pl.ds(768, 768)]),
    ]


def hidden_product(pieces, weight, kind):
    contract = (((1,), (0,)), ((), ())) if kind == "in" else (((1,), (1,)), ((), ()))

    def body(*refs):
        parts, weights, outs = refs[:8], refs[8:11], refs[11:15]
        left, right, done, lsem, rsem, osem = refs[15:]
        x = my_x()

        def rows(t):
            return [(parts[2 * t + k], left.at[t, pl.ds(192 * k, 192), :]) for k in range(2)]

        fetch(weight_parts(kind, weights, right), rsem)
        fetch(rows(0), lsem.at[0])
        arrived(right, rsem)
        for t in range(1, 4):
            fetch(rows(t), lsem.at[t])

        @pl.loop(0, 4)
        def _(t):
            arrived(left.at[t], lsem.at[t])
            done[t] = lax.dot_general(left[t], right[...], contract, preferred_element_type=f32).astype(bf16)
            for i in range(4):

                @pl.when(t ^ x == i)
                def _():
                    pltpu.make_async_copy(done.at[t], outs[i], osem.at[i]).start()

        for i in range(4):
            pltpu.make_async_copy(done.at[i], outs[i], osem.at[i]).wait()

    wshape = (1536, 768) if kind == "in" else (768, 1536)
    return call(
        body,
        [*pieces, *weight],
        [jax.ShapeDtypeStruct((384, 768), bf16)] * 4,
        [
            pltpu.VMEM((4, 384, 1536), bf16),
            pltpu.VMEM(wshape, bf16),
            pltpu.VMEM((4, 384, 768), bf16),
            pltpu.SemaphoreType.DMA((4,)),
            pltpu.SemaphoreType.DMA,
            pltpu.SemaphoreType.DMA((4,)),
        ],
        2 * 1536 * 1536 * 768,
    )


def width_product(hidden, weight, kind, core, got=None):
    contract = (((1,), (1,)), ((), ())) if kind == "in" else (((1,), (0,)), ((), ()))
    flat = [part for piece in hidden for part in piece]
    count = len(flat)
    cols = 768 * 4 // count
    args = [*flat, *weight]
    split = got is not None
    if got is not None:
        args.append(got)

    def body(*refs):
        sources, weights = refs[:count], refs[count : count + 3]
        refs = refs[count + 3 :]
        if got is not None:
            more, refs = refs[0], refs[1:]
        outs, (left, right, done, extra, lsem, rsem, osem, esem) = refs[:-8], refs[-8:]
        x = my_x()

        def rows(j):
            return [
                (sources[j * (count // 4) + n].at[pl.ds(192 * core, 192), :], left.at[j, :, pl.ds(cols * n, cols)])
                for n in range(count // 4)
            ]

        fetch(weight_parts(kind, weights, right), rsem)
        fetch(rows(0), lsem.at[0])
        arrived(right, rsem)
        for j in range(1, 4):
            fetch(rows(j), lsem.at[j])
        if got is not None:
            for j in range(4):
                fetch([(more.at[x ^ j], extra.at[j])], esem.at[j])

        def store(j, x):
            if split:
                for i in range(4):

                    @pl.when(j ^ x == i)
                    def _():
                        pltpu.make_async_copy(done.at[j], outs[i], osem.at[i]).start()
            else:
                pltpu.make_async_copy(done.at[j], outs[0].at[x ^ j], osem.at[j]).start()

        @pl.loop(0, 4)
        def _(j):
            arrived(left.at[j], lsem.at[j])
            total = lax.dot_general(left[j], right[...], contract, preferred_element_type=f32)
            if got is not None:
                arrived(extra.at[j], esem.at[j])
                total = total + extra[j].astype(f32)
            done[j] = total.astype(bf16)
            store(j, x)

        if split:
            for i in range(4):
                pltpu.make_async_copy(done.at[i], outs[i], osem.at[i]).wait()
        else:
            for j in range(4):
                pltpu.make_async_copy(done.at[j], outs[0].at[x ^ j], osem.at[j]).wait()

    wshape = (1536, 768) if kind == "in" else (768, 1536)
    return call(
        body,
        args,
        [jax.ShapeDtypeStruct((192, 1536), bf16)] * 4 if split else [jax.ShapeDtypeStruct((4, 192, 1536), bf16)],
        [
            pltpu.VMEM((4, 192, 768), bf16),
            pltpu.VMEM(wshape, bf16),
            pltpu.VMEM((4, 192, 1536), bf16),
            pltpu.VMEM((4, 192, 1536), bf16),
            pltpu.SemaphoreType.DMA((4,)),
            pltpu.SemaphoreType.DMA,
            pltpu.SemaphoreType.DMA((4,)),
            pltpu.SemaphoreType.DMA((4,)),
        ],
        1536 * 1536 * 768,
    )


def weight_product(pieces, hidden):
    cols = hidden[0].shape[1]
    contract = (((0,), (0,)), ((), ()))
    tile = 256

    def body(*refs):
        parts, sources, outs = refs[:8], refs[8:12], refs[12:14]
        wide, slim, done, wsem, ssem, osem = refs[14:]
        x = my_x()
        fetch([(sources[j], slim.at[pl.ds(pl.multiple_of((x ^ j) * 384, 384), 384), :]) for j in range(4)], ssem)
        fetch([(parts[i], wide.at[pl.ds(192 * i, 192), :]) for i in range(8)], wsem)
        arrived(slim, ssem)
        arrived(wide, wsem)

        def store(t):
            return [
                pltpu.make_async_copy(
                    done.at[t, :, pl.ds(768 * n, 768)],
                    outs[n].at[pl.ds(pl.multiple_of(t * tile, tile), tile), :],
                    osem.at[t, n],
                )
                for n in range(2)
            ]

        count = cols // tile

        @pl.loop(0, count)
        def _(t):
            at = pl.multiple_of(t * tile, tile)
            done[t] = lax.dot_general(
                slim[:, pl.ds(at, tile)], wide[...], contract, preferred_element_type=f32
            ).astype(bf16)
            for copy in store(t):
                copy.start()

        for t in range(count):
            for copy in store(t):
                copy.wait()

    return call(
        body,
        [*pieces, *hidden],
        [jax.ShapeDtypeStruct((cols, 768), bf16)] * 2,
        [
            pltpu.VMEM((1536, 1536), bf16),
            pltpu.VMEM((1536, cols), bf16),
            pltpu.VMEM((cols // tile, tile, 1536), bf16),
            pltpu.SemaphoreType.DMA,
            pltpu.SemaphoreType.DMA,
            pltpu.SemaphoreType.DMA((cols // tile, 2)),
        ],
        2 * 1536 * 1536 * cols,
    )


def turn(pieces):
    tile = 256

    def body(*refs):
        parts, out = refs[:8], refs[8]
        wide, done, wsem, osem = refs[9:]
        fetch([(parts[i], wide.at[pl.ds(192 * i, 192), :]) for i in range(8)], wsem)
        arrived(wide, wsem)

        def store(t):
            return pltpu.make_async_copy(done.at[t], out.at[pl.ds(pl.multiple_of(t * tile, tile), tile), :], osem.at[t])

        @pl.loop(0, 6)
        def _(t):
            done[t] = wide[:, pl.ds(pl.multiple_of(t * tile, tile), tile)].T
            store(t).start()

        for t in range(6):
            store(t).wait()

    return call(
        body,
        list(pieces),
        [jax.ShapeDtypeStruct((1536, 1536), bf16)],
        [
            pltpu.VMEM((1536, 1536), bf16),
            pltpu.VMEM((6, tile, 1536), bf16),
            pltpu.SemaphoreType.DMA,
            pltpu.SemaphoreType.DMA((6,)),
        ],
        0,
    )[0]


def feature_grad(turned, hidden):
    cols = hidden[0].shape[1]
    tile = 256

    def body(*refs):
        source, sources, outs = refs[0], refs[1:5], refs[5:7]
        left, slim, done, lsem, ssem, osem = refs[7:]
        x = my_x()

        def rows(t):
            return [(source.at[pl.ds(((t + 3) % 6) * tile, tile), :], left.at[t])]

        fetch([(sources[j], slim.at[pl.ds(pl.multiple_of((x ^ j) * 384, 384), 384), :]) for j in range(4)], ssem)
        fetch(rows(0), lsem.at[0])
        arrived(slim, ssem)
        for t in range(1, 6):
            fetch(rows(t), lsem.at[t])

        def store(t):
            part = pl.ds((t % 3) * tile, tile)
            return pltpu.make_async_copy(done.at[t], outs[1 if t < 3 else 0].at[part, :], osem.at[t])

        for t in range(6):
            arrived(left.at[t], lsem.at[t])
            done[t] = jnp.dot(left[t], slim[...], preferred_element_type=f32).astype(bf16)
            store(t).start()
        for t in range(6):
            store(t).wait()

    return call(
        body,
        [turned, *hidden],
        [jax.ShapeDtypeStruct((768, cols), bf16)] * 2,
        [
            pltpu.VMEM((6, tile, 1536), bf16),
            pltpu.VMEM((1536, cols), bf16),
            pltpu.VMEM((6, tile, cols), bf16),
            pltpu.SemaphoreType.DMA((6,)),
            pltpu.SemaphoreType.DMA,
            pltpu.SemaphoreType.DMA((6,)),
        ],
        2 * 1536 * 1536 * cols,
    )


def place_blocks(pieces, shape, axis, half=0, whole=None):
    size = pieces[0].shape[axis]

    def body(*refs):
        parts, (out, hold, isem, osem) = refs[:4], refs[-4:]
        y = my_y()

        def store(i, step):
            at = pl.multiple_of((y ^ step) * 768 + half * size, size)
            target = out.at[pl.ds(at, size), :] if axis == 0 else out.at[:, pl.ds(at, size)]
            return pltpu.make_async_copy(hold.at[i], target, osem.at[i])

        for i in range(4):
            pltpu.make_async_copy(parts[i], hold.at[i], isem.at[i]).start()
        for i, step in enumerate((0, 1, 3, 2)):
            pltpu.make_async_copy(parts[i], hold.at[i], isem.at[i]).wait()
            store(i, step).start()
        for i, step in enumerate((0, 1, 3, 2)):
            store(i, step).wait()

    args = list(pieces) if whole is None else [*pieces, whole]
    return call(
        body,
        args,
        [jax.ShapeDtypeStruct(shape, bf16)],
        [
            pltpu.VMEM((4,) + pieces[0].shape, bf16),
            pltpu.SemaphoreType.DMA((4,)),
            pltpu.SemaphoreType.DMA((4,)),
        ],
        0,
        None if whole is None else {4: 0},
    )[0]


def gather_y(rows):
    a = swap(rows, dy=1)
    b = swap(rows, dy=3)
    d = swap(rows, dy=2)
    return jnp.concatenate(
        [jnp.concatenate([rows, a], 1), jnp.concatenate([d, b], 1)], 0
    )


def gather_z(rows):
    p1, p3, p2 = [swap(rows, dz=j) for j in (1, 3, 2)]
    pieces = []
    for own in (rows, p1, p2, p3):
        pieces += [own, swap(own, dcore=1)]
    return pieces


def reduce_z(total):
    sends = [total[j] for j in (1, 3, 2)]
    parts = [swap(v, dz=j) for v, j in zip(sends, (1, 3, 2))]
    rows = total[0].astype(f32) + sum(p.astype(f32) for p in parts)
    kept = rows[:96, :768]
    sends = [rows[:96, 768:].astype(bf16), rows[96:, 768:].astype(bf16), rows[96:, :768].astype(bf16)]
    got = [swap(v, dy=j) for v, j in zip(sends, (1, 3, 2))]
    return (kept + sum(g.astype(f32) for g in got)).astype(bf16)


def solid(value):
    return lax.optimization_barrier(value)


def plan(tokens, w_in, w_out, cotangent):
    y = my_y()
    y1, y3 = y ^ 1, y ^ 3

    tok_y = gather_y(tokens)
    in_a = swap(lax.dynamic_slice(w_in, (0, y1 * 768), (384, 768)), dy=1)
    in_b = swap(lax.dynamic_slice(w_in, (384, y3 * 768), (384, 768)), dy=3)
    tok = gather_z(tok_y)
    w1 = (w_in, in_a, in_b)
    cot_y = gather_y(cotangent)
    out_a = swap(lax.dynamic_slice(w_out, (y1 * 768, 0), (384, 768)), dy=1)
    out_b = swap(lax.dynamic_slice(w_out, (y3 * 768 + 384, 0), (384, 768)), dy=3)
    cot = gather_z(cot_y)
    w2 = (w_out, out_a, out_b)

    pre = hidden_product(tok, w1, "in")
    got = swap_x(pre)
    turned = turn(tok)
    act_own, slope = gelu_both(sum(v.astype(f32) for v in (pre[0], *got)))
    act_own, slope = solid((act_own.astype(bf16), slope))
    act = [act_own, *swap_x([act_own] * 4)]
    back = hidden_product(cot, w2, "out")
    back_got = swap_x(back)

    near, far = weight_product(cot, act)
    og_a, og_b = swap(far, dy=1), swap(far, dy=3)
    og_d = swap(near, dy=2)
    out_grad = place_blocks((near, og_a, og_b, og_d), (3072, 768), 0)
    hidden = [[v] for v in act]
    got = swap(width_product(hidden, w2, "out", 1)[0], dcore=1)
    mixed = reduce_z(width_product(hidden, w2, "out", 0, got))

    act_grad = sum(v.astype(f32) for v in (back[0], *back_got))
    own = act_grad * slope
    own = solid((own[:, :384].astype(bf16), own[:, 384:].astype(bf16)))
    parts = [[own[h], *swap_x([own[h]] * 4)] for h in range(2)]
    hidden = [[parts[0][j], parts[1][j]] for j in range(4)]
    in_grad = None
    for h in range(2):
        near, far = feature_grad(turned, parts[h])
        ig_a, ig_b = swap(far, dy=1), swap(far, dy=3)
        ig_d = swap(near, dy=2)
        in_grad = place_blocks((near, ig_a, ig_b, ig_d), (768, 3072), 1, h, in_grad)
    got = swap(width_product(hidden, w1, "in", 1)[0], dcore=1)
    token_grad = reduce_z(width_product(hidden, w1, "in", 0, got))
    return mixed, token_grad, in_grad, out_grad


def solution(mesh):
    rows = P(("cuts", "fsdp"), "tensor")
    specs = (rows, P("tensor", "fsdp"), P("fsdp", "tensor"), rows)
    outs = (rows, rows, P("tensor", "fsdp"), P("fsdp", "tensor"))
    return jax.shard_map(plan, mesh=mesh, in_specs=specs, out_specs=outs, check_vma=False)
```

```python
import jax
import jax.numpy as jnp
from jax import lax
from jax.experimental import pallas as pl
from jax.experimental.pallas import tpu as pltpu
from jax.sharding import PartitionSpec as P


root_coef = 0.7978845608
cube_coef = 0.044715
AXES = ("cuts", "fsdp", "tensor")
bf16 = jnp.bfloat16
f32 = jnp.float32


def place(index):
    c, rest = divmod(index, 64)
    f, t = divmod(rest, 8)
    x, low = divmod(t, 2)
    z, core = divmod(f, 2)
    return x, 2 * c + low, z, core


def index_of(x, y, z, core):
    return (y // 2) * 64 + (2 * z + core) * 8 + 2 * x + y % 2


def partner(dx=0, dy=0, dz=0, dcore=0):
    pairs = []
    for i in range(128):
        x, y, z, core = place(i)
        pairs.append((i, index_of(x ^ dx, y ^ dy, z ^ dz, core ^ dcore)))
    return pairs


def swap(value, **step):
    return lax.ppermute(value, AXES, partner(**step))


def swap_x(values):
    got = {j: swap(values[j], dx=j) for j in (1, 3, 2)}
    return [got[j] for j in (1, 2, 3)]


def gelu_both(pre_act):
    tanh_part = jnp.tanh(root_coef * (pre_act + cube_coef * pre_act * pre_act * pre_act))
    value = 0.5 * pre_act * (1.0 + tanh_part)
    slope = 0.5 * (1.0 + tanh_part) + 0.5 * pre_act * (1.0 - tanh_part * tanh_part) * root_coef * (
        1.0 + 3.0 * cube_coef * pre_act * pre_act
    )
    return value, slope


def my_y():
    return 2 * lax.axis_index("cuts") + lax.axis_index("tensor") % 2


def my_x():
    return lax.axis_index("tensor") // 2


HBM = pl.BlockSpec(memory_space=pltpu.HBM)


def call(body, args, outs, scratch, flops, aliases=None):
    size = sum(v.size * 2 for v in (*args, *outs))
    return pl.pallas_call(
        body,
        out_shape=outs,
        in_specs=[HBM] * len(args),
        out_specs=[HBM] * len(outs),
        scratch_shapes=scratch,
        input_output_aliases=aliases or {},
        compiler_params=pltpu.CompilerParams(vmem_limit_bytes=22 * 2**20),
        cost_estimate=pl.CostEstimate(flops=flops, transcendentals=0, bytes_accessed=size),
    )(*args)


def fetch(pairs, sem):
    for source, target in pairs:
        pltpu.make_async_copy(source, target, sem).start()


def arrived(ref, sem):
    pltpu.make_async_copy(ref, ref, sem).wait()


def weight_parts(kind, refs, store):
    whole, a, b = refs
    at = pl.multiple_of(my_y() * 768, 768)
    if kind == "in":
        return [
            (whole.at[:, pl.ds(at, 768)], store.at[pl.ds(0, 768), :]),
            (a, store.at[pl.ds(768, 384), :]),
            (b, store.at[pl.ds(1152, 384), :]),
        ]
    return [
        (whole.at[pl.ds(at, 768), :], store.at[:, pl.ds(0, 768)]),
        (a, store.at[pl.ds(0, 384), pl.ds(768, 768)]),
        (b, store.at[pl.ds(384, 384), pl.ds(768, 768)]),
    ]


def pieces_into(places, refs, flat, t=None):
    return [
        (refs[i].at[pl.ds(first, n), :], flat.at[pl.ds(row, n), pl.ds(col, width)])
        for i, first, n, row, col, width in places
        if t is None or row // 384 == t
    ]


def hidden_product(pieces, weight, kind):
    contract = (((1,), (0,)), ((), ())) if kind == "in" else (((1,), (1,)), ((), ()))
    arrays, places = pieces
    count = len(arrays)

    def body(*refs):
        parts, weights, outs = refs[:count], refs[count : count + 3], refs[count + 3 : count + 11]
        left, right, done, lsem, rsem, osem = refs[count + 11 :]
        x = my_x()
        fetch(weight_parts(kind, weights, right), rsem)
        fetch(pieces_into(places, parts, left, 0), lsem.at[0])
        arrived(right, rsem)
        for t in range(1, 4):
            fetch(pieces_into(places, parts, left, t), lsem.at[t])

        @pl.loop(0, 4)
        def _(t):
            rows = pl.ds(pl.multiple_of(t * 384, 384), 384)
            arrived(left.at[rows, :], lsem.at[t])
            done[t] = lax.dot_general(left[rows, :], right[...], contract, preferred_element_type=f32).astype(bf16)
            for i in range(4):

                @pl.when(t ^ x == i)
                def _():
                    for h in range(2):
                        half = done.at[t, :, pl.ds(384 * h, 384)]
                        pltpu.make_async_copy(half, outs[4 * h + i], osem.at[i, h]).start()

        for i in range(4):
            for h in range(2):
                half = done.at[i, :, pl.ds(384 * h, 384)]
                pltpu.make_async_copy(half, outs[4 * h + i], osem.at[i, h]).wait()

    wshape = (1536, 768) if kind == "in" else (768, 1536)
    return call(
        body,
        [*arrays, *weight],
        [jax.ShapeDtypeStruct((384, 384), bf16)] * 8,
        [
            pltpu.VMEM((1536, 1536), bf16),
            pltpu.VMEM(wshape, bf16),
            pltpu.VMEM((4, 384, 768), bf16),
            pltpu.SemaphoreType.DMA((4,)),
            pltpu.SemaphoreType.DMA,
            pltpu.SemaphoreType.DMA((4, 2)),
        ],
        2 * 1536 * 1536 * 768,
    )


def width_product(hidden, weight, kind, core, got=None):
    contract = (((1,), (1,)), ((), ())) if kind == "in" else (((1,), (0,)), ((), ()))
    flat = [part for piece in hidden for part in piece]
    count = len(flat)
    cols = 768 * 4 // count
    args = [*flat, *weight]
    split = got is not None
    if got is not None:
        args.append(got)

    def body(*refs):
        sources, weights = refs[:count], refs[count : count + 3]
        refs = refs[count + 3 :]
        if got is not None:
            more, refs = refs[0], refs[1:]
        outs, (left, right, done, extra, lsem, rsem, osem, esem) = refs[:-8], refs[-8:]
        x = my_x()

        def block(ref, j):
            return ref.at[j // 2, pl.ds(192 * (j % 2), 192), :]

        def rows(j):
            return [
                (
                    sources[j * (count // 4) + n].at[pl.ds(192 * core, 192), :],
                    left.at[j // 2, pl.ds(192 * (j % 2), 192), pl.ds(cols * n, cols)],
                )
                for n in range(count // 4)
            ]

        fetch(weight_parts(kind, weights, right), rsem)
        fetch(rows(0) + rows(1), lsem.at[0])
        arrived(right, rsem)
        fetch(rows(2) + rows(3), lsem.at[1])
        if got is not None:
            for j in range(4):
                fetch([(more.at[x ^ j], block(extra, j))], esem.at[j // 2])

        @pl.loop(0, 2)
        def _(half):
            arrived(left.at[half], lsem.at[half])
            total = lax.dot_general(left[half], right[...], contract, preferred_element_type=f32)
            if got is not None:
                arrived(extra.at[half], esem.at[half])
                total = total + extra[half].astype(f32)
            done[half] = total.astype(bf16)
            for jj in range(2):
                j = 2 * half + jj
                part = done.at[half, pl.ds(192 * jj, 192), :]
                if split:
                    for i in range(4):

                        @pl.when(j ^ x == i)
                        def _():
                            pltpu.make_async_copy(part, outs[i], osem.at[i]).start()
                else:
                    pltpu.make_async_copy(part, outs[0].at[x ^ j], osem.at[j]).start()

        if split:
            for i in range(4):
                pltpu.make_async_copy(block(done, i), outs[i], osem.at[i]).wait()
        else:
            for j in range(4):
                pltpu.make_async_copy(block(done, j), outs[0].at[x ^ j], osem.at[j]).wait()

    wshape = (1536, 768) if kind == "in" else (768, 1536)
    return call(
        body,
        args,
        [jax.ShapeDtypeStruct((192, 1536), bf16)] * 4 if split else [jax.ShapeDtypeStruct((4, 192, 1536), bf16)],
        [
            pltpu.VMEM((2, 384, 768), bf16),
            pltpu.VMEM(wshape, bf16),
            pltpu.VMEM((2, 384, 1536), bf16),
            pltpu.VMEM((2, 384, 1536), bf16),
            pltpu.SemaphoreType.DMA((4,)),
            pltpu.SemaphoreType.DMA,
            pltpu.SemaphoreType.DMA((4,)),
            pltpu.SemaphoreType.DMA((4,)),
        ],
        1536 * 1536 * 768,
    )


def weight_product(pieces, hidden):
    cols = hidden[0].shape[1]
    contract = (((0,), (0,)), ((), ()))
    tile = 384
    arrays, places = pieces
    count = len(arrays)

    def body(*refs):
        parts, sources, outs = refs[:count], refs[count : count + 4], refs[count + 4 : count + 6]
        wide, slim, done, wsem, ssem, osem = refs[count + 6 :]
        x = my_x()
        fetch([(sources[j], slim.at[pl.ds(pl.multiple_of((x ^ j) * 384, 384), 384), :]) for j in range(4)], ssem)
        fetch(pieces_into(places, parts, wide), wsem)
        arrived(slim, ssem)
        arrived(wide, wsem)

        def store(t):
            return [
                pltpu.make_async_copy(
                    done.at[t, :, pl.ds(768 * n, 768)],
                    outs[n].at[pl.ds(pl.multiple_of(t * tile, tile), tile), :],
                    osem.at[t, n],
                )
                for n in range(2)
            ]

        @pl.loop(0, cols // tile)
        def _(t):
            at = pl.multiple_of(t * tile, tile)
            done[t] = lax.dot_general(
                slim[:, pl.ds(at, tile)], wide[...], contract, preferred_element_type=f32
            ).astype(bf16)
            for copy in store(t):
                copy.start()

        for t in range(cols // tile):
            for copy in store(t):
                copy.wait()

    return call(
        body,
        [*arrays, *hidden],
        [jax.ShapeDtypeStruct((cols, 768), bf16)] * 2,
        [
            pltpu.VMEM((1536, 1536), bf16),
            pltpu.VMEM((1536, cols), bf16),
            pltpu.VMEM((cols // tile, tile, 1536), bf16),
            pltpu.SemaphoreType.DMA,
            pltpu.SemaphoreType.DMA,
            pltpu.SemaphoreType.DMA((cols // tile, 2)),
        ],
        2 * 1536 * 1536 * cols,
    )


def turn(pieces):
    tile = 256
    arrays, places = pieces
    count = len(arrays)

    def body(*refs):
        parts, out = refs[:count], refs[count]
        wide, done, wsem, osem = refs[count + 1 :]
        fetch(pieces_into(places, parts, wide), wsem)
        arrived(wide, wsem)

        def store(t):
            return pltpu.make_async_copy(done.at[t], out.at[pl.ds(pl.multiple_of(t * tile, tile), tile), :], osem.at[t])

        @pl.loop(0, 6)
        def _(t):
            done[t] = wide[:, pl.ds(pl.multiple_of(t * tile, tile), tile)].T
            store(t).start()

        for t in range(6):
            store(t).wait()

    return call(
        body,
        list(arrays),
        [jax.ShapeDtypeStruct((1536, 1536), bf16)],
        [
            pltpu.VMEM((1536, 1536), bf16),
            pltpu.VMEM((6, tile, 1536), bf16),
            pltpu.SemaphoreType.DMA,
            pltpu.SemaphoreType.DMA((6,)),
        ],
        0,
    )[0]


def feature_grad(turned, hidden):
    cols = hidden[0].shape[1]
    tile = 384

    def body(*refs):
        source, sources, outs = refs[0], refs[1:5], refs[5:7]
        left, slim, done, lsem, ssem, osem = refs[7:]
        x = my_x()

        def rows(t):
            return [(source.at[pl.ds(((t + 2) % 4) * tile, tile), :], left.at[t])]

        fetch([(sources[j], slim.at[pl.ds(pl.multiple_of((x ^ j) * 384, 384), 384), :]) for j in range(4)], ssem)
        fetch(rows(0), lsem.at[0])
        arrived(slim, ssem)
        for t in range(1, 4):
            fetch(rows(t), lsem.at[t])

        def store(t, far):
            part = pl.ds(pl.multiple_of(lax.rem(t, 2) * tile, tile), tile)
            return pltpu.make_async_copy(done.at[t], outs[far].at[part, :], osem.at[t])

        @pl.loop(0, 4)
        def _(t):
            arrived(left.at[t], lsem.at[t])
            done[t] = jnp.dot(left[t], slim[...], preferred_element_type=f32).astype(bf16)
            pl.when(t < 2)(lambda: store(t, 1).start())
            pl.when(t >= 2)(lambda: store(t, 0).start())

        for t in range(4):
            store(t, 1 if t < 2 else 0).wait()

    return call(
        body,
        [turned, *hidden],
        [jax.ShapeDtypeStruct((768, cols), bf16)] * 2,
        [
            pltpu.VMEM((4, tile, 1536), bf16),
            pltpu.VMEM((1536, cols), bf16),
            pltpu.VMEM((4, tile, cols), bf16),
            pltpu.SemaphoreType.DMA((4,)),
            pltpu.SemaphoreType.DMA,
            pltpu.SemaphoreType.DMA((4,)),
        ],
        2 * 1536 * 1536 * cols,
    )


def place_blocks(pieces, shape, axis, half=0, whole=None):
    size = pieces[0].shape[axis]

    def body(*refs):
        parts, (out, hold, isem, osem) = refs[:4], refs[-4:]
        y = my_y()

        def store(i, step):
            at = pl.multiple_of((y ^ step) * 768 + half * size, size)
            target = out.at[pl.ds(at, size), :] if axis == 0 else out.at[:, pl.ds(at, size)]
            return pltpu.make_async_copy(hold.at[i], target, osem.at[i])

        for i in range(4):
            pltpu.make_async_copy(parts[i], hold.at[i], isem.at[i]).start()
        for i, step in enumerate((0, 1, 3, 2)):
            pltpu.make_async_copy(parts[i], hold.at[i], isem.at[i]).wait()
            store(i, step).start()
        for i, step in enumerate((0, 1, 3, 2)):
            store(i, step).wait()

    args = list(pieces) if whole is None else [*pieces, whole]
    return call(
        body,
        args,
        [jax.ShapeDtypeStruct(shape, bf16)],
        [
            pltpu.VMEM((4,) + pieces[0].shape, bf16),
            pltpu.SemaphoreType.DMA((4,)),
            pltpu.SemaphoreType.DMA((4,)),
        ],
        0,
        None if whole is None else {4: 0},
    )[0]


def gather_y(rows):
    a = swap(rows, dy=1)
    b = swap(rows, dy=3)
    d = swap(rows, dy=2)
    return a, b, d


def gather_z(rows):
    p1, p3, p2 = [swap(rows, dz=j) for j in (1, 3, 2)]
    pieces = []
    for own in (rows, p1, p2, p3):
        pieces += [own, swap(own, dcore=1)]
    return pieces


def gather(rows, early):
    a, b, d = gather_y(rows)
    places = []
    if early:
        trio = jnp.concatenate([a, b, d], 0)
        arrays = gather_z(rows) + gather_z(trio)
        for i in range(8):
            at = 192 * i
            places += [
                (i, 0, 96, at, 0, 768),
                (8 + i, 0, 96, at, 768, 768),
                (8 + i, 96, 96, at + 96, 768, 768),
                (8 + i, 192, 96, at + 96, 0, 768),
            ]
    else:
        block = jnp.concatenate([jnp.concatenate([rows, a], 1), jnp.concatenate([d, b], 1)], 0)
        arrays = gather_z(block)
        places = [(i, 0, 192, 192 * i, 0, 1536) for i in range(8)]
    return arrays, places


def reduce_z(total):
    sends = [total[j] for j in (1, 3, 2)]
    parts = [swap(v, dz=j) for v, j in zip(sends, (1, 3, 2))]
    rows = total[0].astype(f32) + sum(p.astype(f32) for p in parts)
    kept = rows[:96, :768]
    sends = [rows[:96, 768:].astype(bf16), rows[96:, 768:].astype(bf16), rows[96:, :768].astype(bf16)]
    got = [swap(v, dy=j) for v, j in zip(sends, (1, 3, 2))]
    return (kept + sum(g.astype(f32) for g in got)).astype(bf16)


def solid(value):
    return lax.optimization_barrier(value)


def plan(tokens, w_in, w_out, cotangent):
    y = my_y()
    y1, y3 = y ^ 1, y ^ 3

    tok = gather(tokens, True)
    in_a = swap(lax.dynamic_slice(w_in, (0, y1 * 768), (384, 768)), dy=1)
    in_b = swap(lax.dynamic_slice(w_in, (384, y3 * 768), (384, 768)), dy=3)
    w1 = (w_in, in_a, in_b)
    cot = gather(cotangent, False)
    out_a = swap(lax.dynamic_slice(w_out, (y1 * 768, 0), (384, 768)), dy=1)
    out_b = swap(lax.dynamic_slice(w_out, (y3 * 768 + 384, 0), (384, 768)), dy=3)
    w2 = (w_out, out_a, out_b)

    pre = hidden_product(tok, w1, "in")
    terms = [[pre[4 * h], *swap_x(pre[4 * h : 4 * h + 4])] for h in range(2)]
    turned = turn(tok)
    own, slopes = [], []
    for h in range(2):
        value, slope = gelu_both(sum(v.astype(f32) for v in terms[h]))
        value, slope = solid((value.astype(bf16), slope))
        own.append(value)
        slopes.append(slope)
    acts = [[own[h], *swap_x([own[h]] * 4)] for h in range(2)]
    back = hidden_product(cot, w2, "out")
    terms = [[back[4 * h], *swap_x(back[4 * h : 4 * h + 4])] for h in range(2)]

    out_grad = None
    for h in range(2):
        near, far = weight_product(cot, acts[h])
        og_a, og_b = swap(far, dy=1), swap(far, dy=3)
        og_d = swap(near, dy=2)
        out_grad = place_blocks((near, og_a, og_b, og_d), (3072, 768), 0, h, out_grad)
    hidden = [[acts[0][j], acts[1][j]] for j in range(4)]
    got = swap(width_product(hidden, w2, "out", 1)[0], dcore=1)
    mixed = reduce_z(width_product(hidden, w2, "out", 0, got))

    own = []
    for h in range(2):
        act_grad = sum(v.astype(f32) for v in terms[h])
        own.append(solid((act_grad * slopes[h]).astype(bf16)))
    parts = [[own[h], *swap_x([own[h]] * 4)] for h in range(2)]
    hidden = [[parts[0][j], parts[1][j]] for j in range(4)]
    in_grad = None
    for h in range(2):
        near, far = feature_grad(turned, parts[h])
        ig_a, ig_b = swap(far, dy=1), swap(far, dy=3)
        ig_d = swap(near, dy=2)
        in_grad = place_blocks((near, ig_a, ig_b, ig_d), (768, 3072), 1, h, in_grad)
    got = swap(width_product(hidden, w1, "in", 1)[0], dcore=1)
    token_grad = reduce_z(width_product(hidden, w1, "in", 0, got))
    return mixed, token_grad, in_grad, out_grad


def solution(mesh):
    rows = P(("cuts", "fsdp"), "tensor")
    specs = (rows, P("tensor", "fsdp"), P("fsdp", "tensor"), rows)
    outs = (rows, rows, P("tensor", "fsdp"), P("fsdp", "tensor"))
    return jax.shard_map(plan, mesh=mesh, in_specs=specs, out_specs=outs, check_vma=False)
```

```python
import jax
import jax.numpy as jnp
from jax import lax
from jax.experimental import pallas as pl
from jax.experimental.pallas import tpu as pltpu
from jax.sharding import PartitionSpec as P


root_coef = 0.7978845608
cube_coef = 0.044715
AXES = ("cuts", "fsdp", "tensor")
bf16 = jnp.bfloat16
f32 = jnp.float32


def place(index):
    c, rest = divmod(index, 64)
    f, t = divmod(rest, 8)
    x, low = divmod(t, 2)
    z, core = divmod(f, 2)
    return x, 2 * c + low, z, core


def index_of(x, y, z, core):
    return (y // 2) * 64 + (2 * z + core) * 8 + 2 * x + y % 2


def partner(dx=0, dy=0, dz=0, dcore=0):
    pairs = []
    for i in range(128):
        x, y, z, core = place(i)
        pairs.append((i, index_of(x ^ dx, y ^ dy, z ^ dz, core ^ dcore)))
    return pairs


def swap(value, **step):
    return lax.ppermute(value, AXES, partner(**step))


def swap_x(values):
    got = {j: swap(values[j], dx=j) for j in (1, 3, 2)}
    return [got[j] for j in (1, 2, 3)]


def gelu_both(pre_act):
    tanh_part = jnp.tanh(root_coef * (pre_act + cube_coef * pre_act * pre_act * pre_act))
    value = 0.5 * pre_act * (1.0 + tanh_part)
    slope = 0.5 * (1.0 + tanh_part) + 0.5 * pre_act * (1.0 - tanh_part * tanh_part) * root_coef * (
        1.0 + 3.0 * cube_coef * pre_act * pre_act
    )
    return value, slope


def my_y():
    return 2 * lax.axis_index("cuts") + lax.axis_index("tensor") % 2


def my_x():
    return lax.axis_index("tensor") // 2


HBM = pl.BlockSpec(memory_space=pltpu.HBM)


def call(body, args, outs, scratch, flops, aliases=None):
    size = sum(v.size * 2 for v in (*args, *outs))
    return pl.pallas_call(
        body,
        out_shape=outs,
        in_specs=[HBM] * len(args),
        out_specs=[HBM] * len(outs),
        scratch_shapes=scratch,
        input_output_aliases=aliases or {},
        compiler_params=pltpu.CompilerParams(vmem_limit_bytes=22 * 2**20),
        cost_estimate=pl.CostEstimate(flops=flops, transcendentals=0, bytes_accessed=size),
    )(*args)


def fetch(pairs, sem):
    for source, target in pairs:
        pltpu.make_async_copy(source, target, sem).start()


def arrived(ref, sem):
    pltpu.make_async_copy(ref, ref, sem).wait()


def weight_parts(kind, refs, store):
    whole, a, b = refs
    at = pl.multiple_of(my_y() * 768, 768)
    if kind == "in":
        return [
            (whole.at[:, pl.ds(at, 768)], store.at[pl.ds(0, 768), :]),
            (a, store.at[pl.ds(768, 384), :]),
            (b, store.at[pl.ds(1152, 384), :]),
        ]
    return [
        (whole.at[pl.ds(at, 768), :], store.at[:, pl.ds(0, 768)]),
        (a, store.at[pl.ds(0, 384), pl.ds(768, 768)]),
        (b, store.at[pl.ds(384, 384), pl.ds(768, 768)]),
    ]


def pieces_into(places, refs, flat, t=None):
    return [
        (refs[i].at[pl.ds(first, n), :], flat.at[pl.ds(row, n), pl.ds(col, width)])
        for i, first, n, row, col, width in places
        if t is None or row // 384 == t
    ]


def hidden_product(pieces, weight, kind):
    contract = (((1,), (0,)), ((), ())) if kind == "in" else (((1,), (1,)), ((), ()))
    arrays, places = pieces
    count = len(arrays)

    def body(*refs):
        parts, weights, outs = refs[:count], refs[count : count + 3], refs[count + 3 : count + 11]
        left, right, done, lsem, rsem, osem = refs[count + 11 :]
        x = my_x()
        fetch(weight_parts(kind, weights, right), rsem)
        fetch(pieces_into(places, parts, left, 0), lsem.at[0])
        arrived(right, rsem)
        for t in range(1, 4):
            fetch(pieces_into(places, parts, left, t), lsem.at[t])

        @pl.loop(0, 4)
        def _(t):
            rows = pl.ds(pl.multiple_of(t * 384, 384), 384)
            arrived(left.at[rows, :], lsem.at[t])
            done[t] = lax.dot_general(left[rows, :], right[...], contract, preferred_element_type=f32).astype(bf16)
            for i in range(4):

                @pl.when(t ^ x == i)
                def _():
                    for h in range(2):
                        half = done.at[t, :, pl.ds(384 * h, 384)]
                        pltpu.make_async_copy(half, outs[4 * h + i], osem.at[i, h]).start()

        for i in range(4):
            for h in range(2):
                half = done.at[i, :, pl.ds(384 * h, 384)]
                pltpu.make_async_copy(half, outs[4 * h + i], osem.at[i, h]).wait()

    wshape = (1536, 768) if kind == "in" else (768, 1536)
    return call(
        body,
        [*arrays, *weight],
        [jax.ShapeDtypeStruct((384, 384), bf16)] * 8,
        [
            pltpu.VMEM((1536, 1536), bf16),
            pltpu.VMEM(wshape, bf16),
            pltpu.VMEM((4, 384, 768), bf16),
            pltpu.SemaphoreType.DMA((4,)),
            pltpu.SemaphoreType.DMA,
            pltpu.SemaphoreType.DMA((4, 2)),
        ],
        2 * 1536 * 1536 * 768,
    )


def width_product(hidden, weight, kind, core, got=None):
    contract = (((1,), (1,)), ((), ())) if kind == "in" else (((1,), (0,)), ((), ()))
    flat = [part for piece in hidden for part in piece]
    count = len(flat)
    cols = 768 * 4 // count
    args = [*flat, *weight]
    split = got is not None
    if got is not None:
        args.append(got)

    def body(*refs):
        sources, weights = refs[:count], refs[count : count + 3]
        refs = refs[count + 3 :]
        if got is not None:
            more, refs = refs[0], refs[1:]
        outs, (left, right, done, extra, lsem, rsem, osem, esem) = refs[:-8], refs[-8:]
        x = my_x()

        def block(ref, j):
            return ref.at[j // 2, pl.ds(192 * (j % 2), 192), :]

        def rows(j):
            return [
                (
                    sources[j * (count // 4) + n].at[pl.ds(192 * core, 192), :],
                    left.at[j // 2, pl.ds(192 * (j % 2), 192), pl.ds(cols * n, cols)],
                )
                for n in range(count // 4)
            ]

        fetch(weight_parts(kind, weights, right), rsem)
        fetch(rows(0) + rows(1), lsem.at[0])
        arrived(right, rsem)
        fetch(rows(2) + rows(3), lsem.at[1])
        if got is not None:
            for j in range(4):
                fetch([(more.at[x ^ j], block(extra, j))], esem.at[j // 2])

        @pl.loop(0, 4)
        def _(step):
            half, side = step // 2, lax.rem(step, 2)
            wide = pl.ds(pl.multiple_of(side * 768, 768), 768)

            @pl.when(side == 0)
            def _():
                arrived(left.at[half], lsem.at[half])
                if got is not None:
                    arrived(extra.at[half], esem.at[half])

            weights = right[wide, :] if kind == "in" else right[:, wide]
            total = lax.dot_general(left[half], weights, contract, preferred_element_type=f32)
            if got is not None:
                total = total + extra[half, :, wide].astype(f32)
            done[half, :, wide] = total.astype(bf16)

            @pl.when(side == 1)
            def _():
                for jj in range(2):
                    j = 2 * half + jj
                    part = done.at[half, pl.ds(192 * jj, 192), :]
                    if split:
                        for i in range(4):

                            @pl.when(j ^ x == i)
                            def _():
                                pltpu.make_async_copy(part, outs[i], osem.at[i]).start()
                    else:
                        pltpu.make_async_copy(part, outs[0].at[x ^ j], osem.at[j]).start()

        if split:
            for i in range(4):
                pltpu.make_async_copy(block(done, i), outs[i], osem.at[i]).wait()
        else:
            for j in range(4):
                pltpu.make_async_copy(block(done, j), outs[0].at[x ^ j], osem.at[j]).wait()

    wshape = (1536, 768) if kind == "in" else (768, 1536)
    return call(
        body,
        args,
        [jax.ShapeDtypeStruct((192, 1536), bf16)] * 4 if split else [jax.ShapeDtypeStruct((4, 192, 1536), bf16)],
        [
            pltpu.VMEM((2, 384, 768), bf16),
            pltpu.VMEM(wshape, bf16),
            pltpu.VMEM((2, 384, 1536), bf16),
            pltpu.VMEM((2, 384, 1536), bf16),
            pltpu.SemaphoreType.DMA((4,)),
            pltpu.SemaphoreType.DMA,
            pltpu.SemaphoreType.DMA((4,)),
            pltpu.SemaphoreType.DMA((4,)),
        ],
        1536 * 1536 * 768,
    )


def weight_product(pieces, hidden):
    cols = hidden[0].shape[1]
    tile = 384
    arrays, places = pieces
    count = len(arrays)

    def body(*refs):
        parts, sources, outs = refs[:count], refs[count : count + 4], refs[count + 4 : count + 6]
        wide, slim, turned, done, wsem, ssem, osem = refs[count + 6 :]
        x = my_x()
        fetch([(sources[j], slim.at[pl.ds(pl.multiple_of((x ^ j) * 384, 384), 384), :]) for j in range(4)], ssem)
        fetch(pieces_into(places, parts, wide), wsem)
        arrived(slim, ssem)
        arrived(wide, wsem)

        turned[...] = slim[...].T

        def store(n):
            at = pl.ds(pl.multiple_of(lax.rem(n, 2) * tile, tile), tile)
            return [pltpu.make_async_copy(done.at[n], outs[side].at[:, at], osem.at[n]) for side in range(2)]

        @pl.loop(0, 4)
        def _(n):
            at = pl.multiple_of(lax.rem(n + 2, 4) * tile, tile)
            done[n] = jnp.dot(turned[...], wide[:, pl.ds(at, tile)], preferred_element_type=f32).astype(bf16)
            near, far = store(n)
            pl.when(n < 2)(far.start)
            pl.when(n >= 2)(near.start)

        for n in range(4):
            store(n)[n < 2].wait()

    return call(
        body,
        [*arrays, *hidden],
        [jax.ShapeDtypeStruct((cols, 768), bf16)] * 2,
        [
            pltpu.VMEM((1536, 1536), bf16),
            pltpu.VMEM((1536, cols), bf16),
            pltpu.VMEM((cols, 1536), bf16),
            pltpu.VMEM((4, cols, tile), bf16),
            pltpu.SemaphoreType.DMA,
            pltpu.SemaphoreType.DMA,
            pltpu.SemaphoreType.DMA((4,)),
        ],
        2 * 1536 * 1536 * cols,
    )


def turn(pieces):
    tile = 256
    arrays, places = pieces
    count = len(arrays)

    def body(*refs):
        parts, out = refs[:count], refs[count]
        wide, done, wsem, osem = refs[count + 1 :]
        fetch(pieces_into(places, parts, wide), wsem)
        arrived(wide, wsem)

        def store(t):
            return pltpu.make_async_copy(done.at[t], out.at[pl.ds(pl.multiple_of(t * tile, tile), tile), :], osem.at[t])

        @pl.loop(0, 6)
        def _(t):
            done[t] = wide[:, pl.ds(pl.multiple_of(t * tile, tile), tile)].T
            store(t).start()

        for t in range(6):
            store(t).wait()

    return call(
        body,
        list(arrays),
        [jax.ShapeDtypeStruct((1536, 1536), bf16)],
        [
            pltpu.VMEM((1536, 1536), bf16),
            pltpu.VMEM((6, tile, 1536), bf16),
            pltpu.SemaphoreType.DMA,
            pltpu.SemaphoreType.DMA((6,)),
        ],
        0,
    )[0]


def feature_grad(turned, hidden):
    cols = hidden[0].shape[1]
    tile = 384

    def body(*refs):
        source, sources, outs = refs[0], refs[1:5], refs[5:7]
        left, slim, done, lsem, ssem, osem = refs[7:]
        x = my_x()

        def rows(t):
            return [(source.at[pl.ds(((t + 2) % 4) * tile, tile), :], left.at[t])]

        fetch([(sources[j], slim.at[pl.ds(pl.multiple_of((x ^ j) * 384, 384), 384), :]) for j in range(4)], ssem)
        fetch(rows(0), lsem.at[0])
        arrived(slim, ssem)
        for t in range(1, 4):
            fetch(rows(t), lsem.at[t])

        def store(t, far):
            part = pl.ds(pl.multiple_of(lax.rem(t, 2) * tile, tile), tile)
            return pltpu.make_async_copy(done.at[t], outs[far].at[part, :], osem.at[t])

        @pl.loop(0, 4)
        def _(t):
            arrived(left.at[t], lsem.at[t])
            done[t] = jnp.dot(left[t], slim[...], preferred_element_type=f32).astype(bf16)
            pl.when(t < 2)(lambda: store(t, 1).start())
            pl.when(t >= 2)(lambda: store(t, 0).start())

        for t in range(4):
            store(t, 1 if t < 2 else 0).wait()

    return call(
        body,
        [turned, *hidden],
        [jax.ShapeDtypeStruct((768, cols), bf16)] * 2,
        [
            pltpu.VMEM((4, tile, 1536), bf16),
            pltpu.VMEM((1536, cols), bf16),
            pltpu.VMEM((4, tile, cols), bf16),
            pltpu.SemaphoreType.DMA((4,)),
            pltpu.SemaphoreType.DMA,
            pltpu.SemaphoreType.DMA((4,)),
        ],
        2 * 1536 * 1536 * cols,
    )


def place_blocks(pieces, shape, axis, half=0, whole=None):
    size = pieces[0].shape[axis]

    def body(*refs):
        parts, (out, hold, isem, osem) = refs[:4], refs[-4:]
        y = my_y()

        def store(i, step):
            at = pl.multiple_of((y ^ step) * 768 + half * size, size)
            target = out.at[pl.ds(at, size), :] if axis == 0 else out.at[:, pl.ds(at, size)]
            return pltpu.make_async_copy(hold.at[i], target, osem.at[i])

        for i in range(4):
            pltpu.make_async_copy(parts[i], hold.at[i], isem.at[i]).start()
        for i, step in enumerate((0, 1, 3, 2)):
            pltpu.make_async_copy(parts[i], hold.at[i], isem.at[i]).wait()
            store(i, step).start()
        for i, step in enumerate((0, 1, 3, 2)):
            store(i, step).wait()

    args = list(pieces) if whole is None else [*pieces, whole]
    return call(
        body,
        args,
        [jax.ShapeDtypeStruct(shape, bf16)],
        [
            pltpu.VMEM((4,) + pieces[0].shape, bf16),
            pltpu.SemaphoreType.DMA((4,)),
            pltpu.SemaphoreType.DMA((4,)),
        ],
        0,
        None if whole is None else {4: 0},
    )[0]


def gather_y(rows):
    a = swap(rows, dy=1)
    b = swap(rows, dy=3)
    d = swap(rows, dy=2)
    return a, b, d


def gather_z(rows):
    p1, p3, p2 = [swap(rows, dz=j) for j in (1, 3, 2)]
    pieces = []
    for own in (rows, p1, p2, p3):
        pieces += [own, swap(own, dcore=1)]
    return pieces


def gather(rows, early):
    a, b, d = gather_y(rows)
    places = []
    if early:
        trio = jnp.concatenate([a, b, d], 0)
        arrays = gather_z(rows) + gather_z(trio)
        for i in range(8):
            at = 192 * i
            places += [
                (i, 0, 96, at, 0, 768),
                (8 + i, 0, 96, at, 768, 768),
                (8 + i, 96, 96, at + 96, 768, 768),
                (8 + i, 192, 96, at + 96, 0, 768),
            ]
    else:
        block = jnp.concatenate([jnp.concatenate([rows, a], 1), jnp.concatenate([d, b], 1)], 0)
        arrays = gather_z(block)
        places = [(i, 0, 192, 192 * i, 0, 1536) for i in range(8)]
    return arrays, places


def reduce_z(total):
    sends = [total[j] for j in (1, 3, 2)]
    parts = [swap(v, dz=j) for v, j in zip(sends, (1, 3, 2))]
    rows = total[0].astype(f32) + sum(p.astype(f32) for p in parts)
    kept = rows[:96, :768]
    sends = [rows[:96, 768:].astype(bf16), rows[96:, 768:].astype(bf16), rows[96:, :768].astype(bf16)]
    got = [swap(v, dy=j) for v, j in zip(sends, (1, 3, 2))]
    return (kept + sum(g.astype(f32) for g in got)).astype(bf16)


def solid(value):
    return lax.optimization_barrier(value)


def plan(tokens, w_in, w_out, cotangent):
    y = my_y()
    y1, y3 = y ^ 1, y ^ 3

    tok = gather(tokens, True)
    in_a = swap(lax.dynamic_slice(w_in, (0, y1 * 768), (384, 768)), dy=1)
    in_b = swap(lax.dynamic_slice(w_in, (384, y3 * 768), (384, 768)), dy=3)
    w1 = (w_in, in_a, in_b)
    cot = gather(cotangent, False)
    out_a = swap(lax.dynamic_slice(w_out, (y1 * 768, 0), (384, 768)), dy=1)
    out_b = swap(lax.dynamic_slice(w_out, (y3 * 768 + 384, 0), (384, 768)), dy=3)
    w2 = (w_out, out_a, out_b)

    pre = hidden_product(tok, w1, "in")
    terms = [[pre[4 * h], *swap_x(pre[4 * h : 4 * h + 4])] for h in range(2)]
    turned = turn(tok)
    own, slopes = [], []
    for h in range(2):
        value, slope = gelu_both(sum(v.astype(f32) for v in terms[h]))
        value, slope = solid((value.astype(bf16), slope))
        own.append(value)
        slopes.append(slope)
    acts = [[own[h], *swap_x([own[h]] * 4)] for h in range(2)]
    back = hidden_product(cot, w2, "out")
    terms = [[back[4 * h], *swap_x(back[4 * h : 4 * h + 4])] for h in range(2)]

    out_grad = None
    for h in range(2):
        near, far = weight_product(cot, acts[h])
        og_a, og_b = swap(far, dy=1), swap(far, dy=3)
        og_d = swap(near, dy=2)
        out_grad = place_blocks((near, og_a, og_b, og_d), (3072, 768), 0, h, out_grad)
    hidden = [[acts[0][j], acts[1][j]] for j in range(4)]
    got = swap(width_product(hidden, w2, "out", 1)[0], dcore=1)
    mixed = reduce_z(width_product(hidden, w2, "out", 0, got))

    own = []
    for h in range(2):
        act_grad = sum(v.astype(f32) for v in terms[h])
        own.append(solid((act_grad * slopes[h]).astype(bf16)))
    parts = [[own[h], *swap_x([own[h]] * 4)] for h in range(2)]
    hidden = [[parts[0][j], parts[1][j]] for j in range(4)]
    in_grad = None
    for h in range(2):
        near, far = feature_grad(turned, parts[h])
        ig_a, ig_b = swap(far, dy=1), swap(far, dy=3)
        ig_d = swap(near, dy=2)
        in_grad = place_blocks((near, ig_a, ig_b, ig_d), (768, 3072), 1, h, in_grad)
    got = swap(width_product(hidden, w1, "in", 1)[0], dcore=1)
    token_grad = reduce_z(width_product(hidden, w1, "in", 0, got))
    return mixed, token_grad, in_grad, out_grad


def solution(mesh):
    rows = P(("cuts", "fsdp"), "tensor")
    specs = (rows, P("tensor", "fsdp"), P("fsdp", "tensor"), rows)
    outs = (rows, rows, P("tensor", "fsdp"), P("fsdp", "tensor"))
    return jax.shard_map(plan, mesh=mesh, in_specs=specs, out_specs=outs, check_vma=False)
```
